32 devices in a mesh: blk: 32 (over z, y, x, core).
Axes of the slice: x: 2, y: 2, z: 4, core: 2. Of those that a mesh axis runs over, the one named last changes fastest.
Arguments:
- features: bfloat16 [32768, 128], P('blk'), may hold values from -6 to 6
- lengthscale: float32 [128], replicated, may hold values from 4 to 40
- noise_var: float32 [1], replicated, may hold values from 0.5 to 2
- outputscale: float32 [1], replicated, may hold values from 0.03 to 0.1
- solution: float32 [32768, 64], P('blk'), may hold values from -6 to 6
- residual: float32 [32768, 64], P('blk'), may hold values from -36 to 36
- direction: float32 [32768, 64], P('blk'), may hold values from -36 to 36
Outputs:
- new_solution: float32 [32768, 64], P('blk')
- new_residual: float32 [32768, 64], P('blk')
- new_direction: float32 [32768, 64], P('blk')
The draws below stay inside these ranges and needn't reach their ends.
All inputs are finite; a program needn't handle non-finite values.
Results may differ from the reference program's by a relative error of at most 0.0014.
Values may be sent and summed in bfloat16 or wider, within the bound.
No kernel may reach another device: no remote copies, remote signals or barrier semaphores. Data moves between devices by JAX's collectives and lax.ppermute only.
A program may use at most 64 MiB of HBM per device.

```python
import math
import jax
import jax.numpy as jnp
from jax import lax

FEAT = 128
RHS = 64
PTS_DEV = 1024
NPOINTS = 32768
STRIDE_C = 4
STRIDE_D = 9
N_BLK = 32


def rough_field(key, salt):
    first, second = jax.random.split(jax.random.fold_in(key, salt), 2)
    rising = jnp.linspace(1.0, 3.0, NPOINTS, dtype=jnp.float32)[:, None]
    columns = jnp.exp(jax.random.uniform(second, (1, RHS), jnp.float32, jnp.log(0.3), jnp.log(3.0)))
    base = jnp.clip(jax.random.normal(first, (NPOINTS, RHS), jnp.float32), -4.0, 4.0)
    return base * rising * columns


def draw_residual(key, part):
    return rough_field(key, 11)


def draw_direction(key, part):
    return rough_field(key, 23)


def block_scale(rng, dims, shards, least, top_value):
    level, own = 1.0, jax.random.fold_in(rng, 6)
    for axis_at, shards_of in shards:
        heights = jnp.exp(jax.random.uniform(jax.random.fold_in(own, axis_at), (shards_of,), jnp.float32, least / len(shards), top_value / len(shards)))
        level = level * jnp.repeat(heights, dims[axis_at] // shards_of).reshape([-1 if axis == axis_at else 1 for axis in range(len(dims))])
    return level


def normal_values(own_key, extent, width, most, shards=(), held_as=jnp.bfloat16):
    drawn = jax.random.normal(own_key, extent, jnp.float32) * width
    if len(shards) > 0:
        drawn = block_scale(own_key, extent, shards, -0.22, 0.18) * drawn
    return jnp.clip(drawn, min=-most, max=most).astype(held_as)


def setup_inputs(seed: int = 0) -> dict:
    arg_keys = jax.random.split(jax.random.key(seed), 8)
    return {
        "features": normal_values(arg_keys[0], (NPOINTS, FEAT), 1.0, 6.0, ((0, 32),)),
        "lengthscale": jnp.clip(jnp.exp(jax.random.uniform(arg_keys[1], (FEAT,), jnp.float32, math.log(4.0), math.log(40.0))), 4.0, 40.0),
        "noise_var": jnp.clip(jnp.exp(jax.random.uniform(arg_keys[2], (1,), jnp.float32, math.log(0.5), math.log(2.0))), 0.5, 2.0),
        "outputscale": jnp.clip(jnp.exp(jax.random.uniform(arg_keys[3], (1,), jnp.float32, math.log(0.03), math.log(0.1))), 0.03, 0.1),
        "solution": normal_values(arg_keys[4], (NPOINTS, RHS), 1.0, 6.0, ((0, 32),), jnp.float32),
        "residual": draw_residual(jax.random.fold_in(arg_keys[7], 71), 0),
        "direction": draw_direction(jax.random.fold_in(arg_keys[7], 71), 0),
    }


root_five = math.sqrt(5.0)

def matern(left_points, left_norm, right_points, right_norm, scale):
    inner_products = jnp.dot(left_points, right_points.T, preferred_element_type=jnp.float32)
    squared_range = jnp.maximum(left_norm[:, None] + right_norm[None, :] - 2.0 * inner_products, 0.0)
    scaled_range = root_five * jnp.sqrt(squared_range)
    return scale * (1.0 + scaled_range + scaled_range * scaled_range / 3.0) * jnp.exp(-scaled_range)

def reference(features, lengthscale, noise_var, outputscale, solution, residual, direction):
    highest = lax.Precision.HIGHEST
    scaled = (features.astype(jnp.float32) / lengthscale[None, :]).astype(jnp.bfloat16)
    point_norms = lax.optimization_barrier(jnp.sum(jnp.square(scaled.astype(jnp.float32)), axis=1))
    block_points = scaled.reshape(N_BLK, PTS_DEV, FEAT)
    block_norms = point_norms.reshape(N_BLK, PTS_DEV)
    block_direction = direction.reshape(N_BLK, PTS_DEV, RHS)
    scale = outputscale[0]

    def diagonal_block(pieces):
        own_points, own_norm, own_direction = pieces
        kernel_tile = matern(own_points, own_norm, own_points, own_norm, scale)
        return jnp.dot(kernel_tile, own_direction, precision=highest, preferred_element_type=jnp.float32)

    def pair_block(pieces):
        own_points, own_norm, own_direction, far_points, far_norm, far_direction = pieces
        kernel_tile = matern(own_points, own_norm, far_points, far_norm, scale)
        forward = jnp.dot(kernel_tile, far_direction, precision=highest, preferred_element_type=jnp.float32)
        backward = lax.dot_general(kernel_tile, own_direction, (((0,), (0,)), ((), ())), precision=highest, preferred_element_type=jnp.float32)
        return (forward, backward)
    applied = noise_var[0] * block_direction + lax.map(diagonal_block, (block_points, block_norms, block_direction))
    for offset in (1, 3, STRIDE_C, STRIDE_D):
        forward, backward = lax.map(pair_block, (block_points, block_norms, block_direction, jnp.roll(block_points, -offset, 0), jnp.roll(block_norms, -offset, 0), jnp.roll(block_direction, -offset, 0)))
        applied = applied + forward + jnp.roll(backward, offset, 0)
    applied = applied.reshape(NPOINTS, RHS)
    old_norm = lax.optimization_barrier(jnp.sum(residual * residual, axis=0)) / NPOINTS
    curvature = lax.optimization_barrier(jnp.sum(direction * applied, axis=0)) / NPOINTS
    step_size = old_norm / jnp.maximum(curvature, 1.0)
    new_solution = solution + step_size[None, :] * direction
    new_residual = residual - step_size[None, :] * applied
    updated_norm = lax.optimization_barrier(jnp.sum(new_residual * new_residual, axis=0)) / NPOINTS
    new_direction = new_residual + (updated_norm / (old_norm + 1e-06))[None, :] * direction
    return (new_solution, new_residual, new_direction)
```

```python
import math

import jax
import jax.numpy as jnp
from jax import lax
from jax.experimental import pallas as pl
from jax.experimental.pallas import tpu as pltpu
from jax.sharding import PartitionSpec as P

LANES = 128
ROWS = 256
TINY = 1e-30
root_five = math.sqrt(5.0)
LINEAR = 3.0 / root_five
CONSTANT = 0.6
DECAY = -root_five * math.log2(math.e)


def shape(radius):
    return ((radius + LINEAR) * radius + CONSTANT) * jnp.exp2(radius * DECAY)


def rounded_parts(value):
    high = value.astype(jnp.bfloat16).astype(jnp.float32)
    rest = value - high
    middle = rest.astype(jnp.bfloat16).astype(jnp.float32)
    return high, middle, rest - middle


def lane_parts(value, lanes, first):
    high, middle, low = rounded_parts(value)
    return jnp.where(
        lanes == first,
        high,
        jnp.where(lanes == first + 1, middle, jnp.where(lanes == first + 2, low, 0.0)),
    )


def pack_kernel(features_ref, lengthscale_ref, direction_ref, packed_ref, own_ref, stats_ref):
    points, feat = features_ref.shape
    rhs = direction_ref.shape[0]
    scaled = (features_ref[...].astype(jnp.float32) / lengthscale_ref[...]).astype(jnp.bfloat16)
    packed_ref[:points, :] = scaled
    wide = scaled.astype(jnp.float32)
    norms = jnp.sum(wide * wide, axis=1, keepdims=True)
    lanes = lax.broadcasted_iota(jnp.int32, (points, LANES), 1)
    own_ref[:, :feat] = (-2.0 * wide).astype(jnp.bfloat16)
    own_ref[:, feat:] = lane_parts(norms, lanes, 0).astype(jnp.bfloat16)
    stats_ref[0:1, :] = jnp.sum(wide, axis=0, keepdims=True) / points
    stats_ref[1:2, :] = jnp.broadcast_to(
        jnp.sum(norms, axis=0, keepdims=True) / points, (1, LANES)
    )
    stats_ref[2:, :] = jnp.zeros((stats_ref.shape[0] - 2, LANES), jnp.float32)
    for chunk in range(points // LANES):
        packed_ref[points + chunk * rhs : points + (chunk + 1) * rhs, :] = direction_ref[
            :, chunk * LANES : (chunk + 1) * LANES
        ].astype(jnp.bfloat16)
    totals = jnp.sum(direction_ref[...], axis=1, keepdims=True)
    lanes = lax.broadcasted_iota(jnp.int32, (rhs, LANES), 1)
    packed_ref[packed_ref.shape[0] - rhs :, :] = lane_parts(totals, lanes, 0).astype(jnp.bfloat16)


def tile_kernel(packed_ref, own_ref, stats_ref, sum_ref, out_ref):
    rhs, points = sum_ref.shape
    feat = packed_ref.shape[1]
    far_mean = jnp.zeros((1, feat), jnp.float32)
    far_norm = jnp.zeros((1, 1), jnp.float32)
    norms = []
    for start in range(0, points, ROWS):
        wide = packed_ref[start : start + ROWS, :].astype(jnp.float32)
        norms.append(jnp.sum(wide * wide, axis=1, keepdims=True))
        far_mean = far_mean + jnp.sum(wide, axis=0, keepdims=True)
        far_norm = far_norm + jnp.sum(norms[-1], axis=0, keepdims=True)
    cross = jnp.sum(far_mean * stats_ref[0:1, :], axis=1, keepdims=True)
    mean_range = stats_ref[1:2, 0:1] + (far_norm - 2.0 * cross) / points
    mean_range = jnp.maximum(mean_range, TINY)
    level = shape(mean_range * lax.rsqrt(mean_range))
    totals = jnp.sum(
        packed_ref[packed_ref.shape[0] - rhs :, :].astype(jnp.float32), axis=1, keepdims=True
    )
    out_ref[...] = sum_ref[...] + level * totals
    lanes = lax.broadcasted_iota(jnp.int32, (ROWS, LANES), 1)
    ones = jnp.where(lanes < 3, 1.0, 0.0).astype(jnp.bfloat16)
    for index, start in enumerate(range(0, points, ROWS)):
        far = jnp.concatenate([packed_ref[start : start + ROWS, :], ones], axis=1)
        inner = lax.dot_general(
            far, own_ref[...], (((1,), (1,)), ((), ())), preferred_element_type=jnp.float32
        )
        squared = jnp.maximum(inner + norms[index], TINY)
        tile = (shape(squared * lax.rsqrt(squared)) - level).astype(jnp.bfloat16)
        first = points + start // LANES * rhs
        far_direction = jnp.concatenate(
            [packed_ref[first + k * rhs : first + (k + 1) * rhs, :] for k in range(ROWS // LANES)],
            axis=1,
        )
        out_ref[...] += jnp.dot(far_direction, tile, preferred_element_type=jnp.float32)


def sums_kernel(scalars_ref, sum_ref, direction_ref, residual_ref, applied_ref, sums_ref):
    applied = scalars_ref[0] * direction_ref[...] + (scalars_ref[1] / CONSTANT) * sum_ref[...]
    applied_ref[...] = applied
    residual = residual_ref[...]
    rhs = applied.shape[0]
    columns = [
        jnp.sum(value, axis=1, keepdims=True)
        for value in (
            residual * residual,
            direction_ref[...] * applied,
            residual * applied,
            applied * applied,
        )
    ]
    lanes = lax.broadcasted_iota(jnp.int32, (rhs, LANES), 1)
    table = jnp.zeros((rhs, LANES), jnp.float32)
    for k, column in enumerate(columns):
        table = jnp.where(lanes == k, column, table)
    rows = jnp.concatenate([table, jnp.zeros((LANES - rhs, LANES), jnp.float32)], axis=0).T[:8, :]
    for device in range(sums_ref.shape[0]):
        sums_ref[device] = rows


def update_kernel(
    sums_ref, direction_ref, residual_ref, solution_ref, applied_ref,
    new_solution_ref, new_residual_ref, new_direction_ref,
):
    rhs, points = direction_ref.shape
    total = float(points * sums_ref.shape[0])
    rows = sums_ref[0]
    for device in range(1, sums_ref.shape[0]):
        rows = rows + sums_ref[device]
    rows = rows / total
    table = jnp.concatenate([rows, jnp.zeros((LANES - 8, LANES), jnp.float32)], axis=0).T[:rhs, :]
    old_norm, curvature, cross_term, applied_norm = (table[:, k : k + 1] for k in range(4))
    step_size = old_norm / jnp.maximum(curvature, 1.0)
    updated_norm = old_norm - 2.0 * step_size * cross_term + step_size * step_size * applied_norm
    direction = direction_ref[...]
    new_solution_ref[...] = solution_ref[...] + step_size * direction
    new_residual = residual_ref[...] - step_size * applied_ref[...]
    new_residual_ref[...] = new_residual
    new_direction_ref[...] = new_residual + (updated_norm / (old_norm + 1e-06)) * direction


def in_vmem(count):
    return [pl.BlockSpec(memory_space=pltpu.VMEM)] * count


def local(features, lengthscale, noise_var, outputscale, solution, residual, direction):
    points, feat = features.shape
    rhs = direction.shape[1]
    blocks = lax.axis_size("blk")
    direction, residual, solution = direction.T, residual.T, solution.T
    rows = points + rhs * (points // LANES) + rhs
    packed, own, stats = pl.pallas_call(
        pack_kernel,
        out_shape=(
            jax.ShapeDtypeStruct((rows, feat), jnp.bfloat16),
            jax.ShapeDtypeStruct((points, feat + LANES), jnp.bfloat16),
            jax.ShapeDtypeStruct((8, LANES), jnp.float32),
        ),
        in_specs=in_vmem(3),
        out_specs=tuple(in_vmem(3)),
        name="pack",
    )(features, lengthscale[None, :], direction)

    def moved(block, source_of):
        return lax.ppermute(block, "blk", [(source_of(i), i) for i in range(blocks)])

    def ahead(block, offset):
        return moved(block, lambda i: (i + offset) % blocks)

    stride_c, stride_d = blocks // 8, blocks // 4 + 1
    place = lax.axis_index("blk")
    if stride_c == 1 + 3:
        up_c, down_c = ahead(packed, stride_c), ahead(packed, -stride_c)
        up_d, down_d = ahead(packed, stride_d), ahead(packed, -stride_d)
        beside = moved(packed, lambda i: i ^ 3)
        partner = moved(packed, lambda i: i ^ 1)
        on_chip = moved(jnp.where(place % 2 == 0, up_c, down_c), lambda i: i ^ 1)
        next_chip = moved(jnp.where(place // 2 % 2 == 0, up_c, down_c), lambda i: i ^ 3)
        arrivals = (partner, beside, up_c, down_c, on_chip, up_d, down_d, next_chip)
    else:
        arrivals = tuple(
            ahead(packed, sign * offset)
            for offset in (1, 3, stride_c, stride_d)
            for sign in (1, -1)
        )
    acc = jnp.zeros((rhs, points), jnp.float32)
    for block in (packed, *arrivals):
        acc = pl.pallas_call(
            tile_kernel,
            out_shape=jax.ShapeDtypeStruct((rhs, points), jnp.float32),
            in_specs=in_vmem(4),
            out_specs=in_vmem(1)[0],
            cost_estimate=pl.CostEstimate(
                flops=2 * points * points * (feat + LANES + rhs),
                bytes_accessed=rows * feat * 2,
                transcendentals=2 * points * points,
            ),
            name="tile",
        )(block, own, stats, acc)
    applied, sums = pl.pallas_call(
        sums_kernel,
        out_shape=(
            jax.ShapeDtypeStruct((rhs, points), jnp.float32),
            jax.ShapeDtypeStruct((blocks, 8, LANES), jnp.float32),
        ),
        in_specs=[pl.BlockSpec(memory_space=pltpu.SMEM)] + in_vmem(3),
        out_specs=tuple(in_vmem(2)),
        name="sums",
    )(jnp.concatenate([noise_var, outputscale]), acc, direction, residual)
    sums = lax.all_to_all(sums, "blk", 0, 0, tiled=False)
    outputs = pl.pallas_call(
        update_kernel,
        out_shape=(jax.ShapeDtypeStruct((rhs, points), jnp.float32),) * 3,
        in_specs=in_vmem(5),
        out_specs=tuple(in_vmem(3)),
        name="update",
    )(sums, direction, residual, solution, applied)
    return tuple(output.T for output in outputs)


def solution(mesh):
    return jax.shard_map(
        local,
        mesh=mesh,
        in_specs=(P("blk", None), P(), P(), P(), P("blk", None), P("blk", None), P("blk", None)),
        out_specs=(P("blk", None), P("blk", None), P("blk", None)),
        check_vma=False,
    )
```

```python
import math

import jax
import jax.numpy as jnp
from jax import lax
from jax.experimental import pallas as pl
from jax.experimental.pallas import tpu as pltpu
from jax.sharding import PartitionSpec as P


LANES = 128
TINY = 1e-30
root_five = math.sqrt(5.0)
LINEAR = 3.0 / root_five
CONSTANT = 0.6


def shape(radius):
    return ((radius + LINEAR) * radius + CONSTANT) * jnp.exp(radius * -root_five)


def rounded_parts(value):
    high = value.astype(jnp.bfloat16).astype(jnp.float32)
    rest = value - high
    middle = rest.astype(jnp.bfloat16).astype(jnp.float32)
    return high, middle, rest - middle


def lane_parts(value, lanes, first):
    high, middle, low = rounded_parts(value)
    return jnp.where(
        lanes == first,
        high,
        jnp.where(lanes == first + 1, middle, jnp.where(lanes == first + 2, low, 0.0)),
    )


def pack_kernel(features_ref, lengthscale_ref, direction_ref, packed_ref, own_ref, stats_ref):
    points, feat = features_ref.shape
    rhs = direction_ref.shape[0]
    scaled = (features_ref[...].astype(jnp.float32) / lengthscale_ref[...]).astype(jnp.bfloat16)
    packed_ref[:points, :] = scaled
    wide = scaled.astype(jnp.float32)
    norms = jnp.sum(wide * wide, axis=1, keepdims=True)
    lanes = lax.broadcasted_iota(jnp.int32, (points, LANES), 1)
    own_ref[:, :feat] = (-2.0 * wide).astype(jnp.bfloat16)
    own_ref[:, feat:] = lane_parts(norms, lanes, 0).astype(jnp.bfloat16)
    stats_ref[0:1, :] = jnp.sum(wide, axis=0, keepdims=True) / points
    stats_ref[1:2, :] = jnp.broadcast_to(
        jnp.sum(norms, axis=0, keepdims=True) / points, (1, LANES)
    )
    stats_ref[2:, :] = jnp.zeros((stats_ref.shape[0] - 2, LANES), jnp.float32)
    for chunk in range(points // LANES):
        packed_ref[points + chunk * rhs : points + (chunk + 1) * rhs, :] = direction_ref[
            :, chunk * LANES : (chunk + 1) * LANES
        ].astype(jnp.bfloat16)
    totals = jnp.sum(direction_ref[...], axis=1, keepdims=True)
    lanes = lax.broadcasted_iota(jnp.int32, (rhs, LANES), 1)
    packed_ref[packed_ref.shape[0] - rhs :, :] = lane_parts(totals, lanes, 0).astype(jnp.bfloat16)


def tile_kernel(packed_ref, own_ref, stats_ref, sum_ref, out_ref):
    rhs, points = sum_ref.shape
    far = packed_ref[:points, :]
    wide = far.astype(jnp.float32)
    norms = jnp.sum(wide * wide, axis=1, keepdims=True)
    far_mean = jnp.sum(wide, axis=0, keepdims=True)
    far_norm = jnp.sum(norms, axis=0, keepdims=True)
    cross = jnp.sum(far_mean * stats_ref[0:1, :], axis=1, keepdims=True)
    mean_range = stats_ref[1:2, 0:1] + (far_norm - 2.0 * cross) / points
    mean_range = jnp.maximum(mean_range, TINY)
    level = shape(mean_range * lax.rsqrt(mean_range))
    totals = jnp.sum(
        packed_ref[packed_ref.shape[0] - rhs :, :].astype(jnp.float32), axis=1, keepdims=True
    )
    lanes = lax.broadcasted_iota(jnp.int32, (points, LANES), 1)
    ones = jnp.where(lanes < 3, 1.0, 0.0).astype(jnp.bfloat16)
    inner = lax.dot_general(
        jnp.concatenate([far, ones], axis=1),
        own_ref[...],
        (((1,), (1,)), ((), ())),
        preferred_element_type=jnp.float32,
    )
    squared = jnp.maximum(inner + norms, TINY)
    tile = (shape(squared * lax.rsqrt(squared)) - level).astype(jnp.bfloat16)
    far_direction = jnp.concatenate(
        [
            packed_ref[points + k * rhs : points + (k + 1) * rhs, :]
            for k in range(points // LANES)
        ],
        axis=1,
    )
    product = jnp.dot(far_direction, tile, preferred_element_type=jnp.float32)
    out_ref[...] = sum_ref[...] + level * totals + product


def sums_kernel(noise_ref, scale_ref, sum_ref, direction_ref, residual_ref, applied_ref, sums_ref):
    applied = noise_ref[0] * direction_ref[...] + (scale_ref[0] / CONSTANT) * sum_ref[...]
    applied_ref[...] = applied
    residual = residual_ref[...]
    rhs = applied.shape[0]
    columns = [
        jnp.sum(value, axis=1, keepdims=True)
        for value in (
            residual * residual,
            direction_ref[...] * applied,
            residual * applied,
            applied * applied,
        )
    ]
    lanes = lax.broadcasted_iota(jnp.int32, (rhs, LANES), 1)
    table = jnp.zeros((rhs, LANES), jnp.float32)
    for k, column in enumerate(columns):
        table = jnp.where(lanes == k, column, table)
    rows = jnp.concatenate([table, jnp.zeros((LANES - rhs, LANES), jnp.float32)], axis=0).T[:8, :]
    for device in range(sums_ref.shape[0]):
        sums_ref[device] = rows


def update_kernel(
    sums_ref, direction_ref, residual_ref, solution_ref, applied_ref,
    new_solution_ref, new_residual_ref, new_direction_ref,
):
    rhs, points = direction_ref.shape
    total = float(points * sums_ref.shape[0])
    rows = sums_ref[0]
    for device in range(1, sums_ref.shape[0]):
        rows = rows + sums_ref[device]
    rows = rows / total
    table = jnp.concatenate([rows, jnp.zeros((LANES - 8, LANES), jnp.float32)], axis=0).T[:rhs, :]
    old_norm, curvature, cross_term, applied_norm = (table[:, k : k + 1] for k in range(4))
    step_size = old_norm / jnp.maximum(curvature, 1.0)
    updated_norm = old_norm - 2.0 * step_size * cross_term + step_size * step_size * applied_norm
    direction = direction_ref[...]
    new_solution_ref[...] = solution_ref[...] + step_size * direction
    new_residual = residual_ref[...] - step_size * applied_ref[...]
    new_residual_ref[...] = new_residual
    new_direction_ref[...] = new_residual + (updated_norm / (old_norm + 1e-06)) * direction


def resident(array):
    return pltpu.with_memory_space_constraint(array, pltpu.VMEM)


def grant(mebibytes):
    return pltpu.CompilerParams(vmem_limit_bytes=mebibytes * 1024 * 1024)


def in_vmem(count):
    return [pl.BlockSpec(memory_space=pltpu.VMEM)] * count


def local(features, lengthscale, noise_var, outputscale, solution, residual, direction):
    points, feat = features.shape
    rhs = direction.shape[1]
    blocks = lax.axis_size("blk")
    direction, residual, solution = direction.T, residual.T, solution.T
    rows = points + rhs * (points // LANES) + rhs
    packed, own, stats = pl.pallas_call(
        pack_kernel,
        out_shape=(
            pltpu.VMEM((rows, feat), jnp.bfloat16),
            pltpu.VMEM((points, feat + LANES), jnp.bfloat16),
            pltpu.VMEM((8, LANES), jnp.float32),
        ),
        in_specs=in_vmem(3),
        out_specs=tuple(in_vmem(3)),
        compiler_params=grant(8),
        name="pack",
    )(features, lengthscale[None, :], direction)

    def moved(block, source_of):
        return lax.ppermute(block, "blk", [(source_of(i), i) for i in range(blocks)])

    def ahead(block, offset):
        return moved(block, lambda i: (i + offset) % blocks)

    def accumulate(acc, *arrived):
        for block in arrived:
            acc = pl.pallas_call(
                tile_kernel,
                out_shape=pltpu.VMEM((rhs, points), jnp.float32),
                in_specs=in_vmem(4),
                out_specs=in_vmem(1)[0],
                cost_estimate=pl.CostEstimate(
                    flops=2 * points * points * (feat + LANES + rhs),
                    bytes_accessed=rows * feat * 2,
                    transcendentals=2 * points * points,
                ),
                compiler_params=grant(16),
                name="tile",
            )(*map(resident, (block, own, stats, acc)))
        return acc

    stride_c, stride_d = blocks // 8, blocks // 4 + 1
    place = lax.axis_index("blk")
    acc = jnp.zeros((rhs, points), jnp.float32)
    if stride_c == 1 + 3:
        up_d = ahead(packed, stride_d)
        down_d = ahead(packed, -stride_d)
        up_c = ahead(packed, stride_c)
        down_c = ahead(packed, -stride_c)
        beside = moved(packed, lambda i: i ^ 3)
        partner = moved(packed, lambda i: i ^ 1)
        acc = accumulate(acc, packed)
        acc = accumulate(acc, partner, beside)
        acc, up_c, down_c = lax.optimization_barrier((acc, up_c, down_c))
        on_chip = moved(jnp.where(place % 2 == 0, up_c, down_c), lambda i: i ^ 1)
        next_chip = moved(jnp.where(place // 2 % 2 == 0, up_c, down_c), lambda i: i ^ 3)
        acc = accumulate(acc, up_c, down_c, on_chip, next_chip, up_d, down_d)
    else:
        arrivals = tuple(
            ahead(packed, sign * offset)
            for offset in (1, 3, stride_c, stride_d)
            for sign in (1, -1)
        )
        acc = accumulate(acc, packed, *arrivals)
    applied, sums = pl.pallas_call(
        sums_kernel,
        out_shape=(
            pltpu.VMEM((rhs, points), jnp.float32),
            pltpu.VMEM((blocks, 8, LANES), jnp.float32),
        ),
        in_specs=[pl.BlockSpec(memory_space=pltpu.SMEM)] * 2 + in_vmem(3),
        out_specs=tuple(in_vmem(2)),
        compiler_params=grant(8),
        name="sums",
    )(noise_var, outputscale, *map(resident, (acc, direction, residual)))
    sums = lax.all_to_all(sums, "blk", 0, 0, tiled=False)
    outputs = pl.pallas_call(
        update_kernel,
        out_shape=(jax.ShapeDtypeStruct((rhs, points), jnp.float32),) * 3,
        in_specs=in_vmem(5),
        out_specs=tuple(in_vmem(3)),
        compiler_params=grant(8),
        name="update",
    )(*map(resident, (sums, direction, residual, solution, applied)))
    return tuple(output.T for output in outputs)


def solution(mesh):
    return jax.shard_map(
        local,
        mesh=mesh,
        in_specs=(P("blk", None), P(), P(), P(), P("blk", None), P("blk", None), P("blk", None)),
        out_specs=(P("blk", None), P("blk", None), P("blk", None)),
        check_vma=False,
    )
```
